128 devices in a mesh: row: 16 (over x, z_lo, core), col: 8 (over z_hi, y).
Axes of the slice: x: 4, y: 4, z: 4 (z_hi: 2, z_lo: 2; z = z_hi * 2 + z_lo), core: 2. Of those that a mesh axis runs over, the one named last changes fastest.
Arguments:
- t_amps: float32 [8192, 8192], P('row', 'col'), may hold values from -0.05 to 0.05
- cholesky: float32 [8192, 2048], P(('row', 'col')), may hold values from -0.79549515 to 0.79549515
- eps_occ: float32 [8], replicated, may hold values from -2 to -0.3
- eps_vir: float32 [1024], replicated, may hold values from 0.2 to 4
Outputs:
- t_new: float32 [8192, 8192], P('row', 'col')
The draws below stay inside these ranges and needn't reach their ends.
All inputs are finite; a program needn't handle non-finite values.
Results may differ from the reference program's by a relative error of at most 0.000088.
Values sent between devices are 32-bit elements; how exact they have to be, the bound alone decides.
A program may use at most 64 MiB of HBM per device.

```python
import jax
import jax.numpy as jnp
from jax import lax

OCC = 8
VIR = 1024
CHOL = 2048
OV = 8192
N_ROW = 16
N_COL = 8


def levels(own_key, extent, cuts, least, largest):
    gain = 1.0
    for dim, shards_of in cuts:
        steps = jax.random.uniform(jax.random.fold_in(jax.random.fold_in(own_key, 6), dim), (shards_of,), jnp.float32, least / len(cuts), largest / len(cuts))
        gain = gain * jnp.repeat(jnp.exp(steps), extent[dim] // shards_of).reshape((-1,) + (1,) * (len(extent) - 1 - dim))
    return gain


def gaussian(own_key, extent, deviation, most, shards=(), kind=jnp.bfloat16):
    level = levels(own_key, extent, shards, -0.22, 0.18) if shards else 1.0
    values = jax.random.normal(own_key, extent, jnp.float32) * deviation * level
    return jnp.minimum(jnp.maximum(values, -most), most).astype(kind)


def setup_inputs(seed: int = 0) -> dict:
    splits = jax.random.split(jax.random.key(seed), 5)
    return {
        "t_amps": gaussian(splits[0], (OV, OV), 0.008, 0.05, ((0, 16), (1, 8)), jnp.float32),
        "cholesky": gaussian(splits[1], (OV, CHOL), (4.5 * CHOL ** -0.5), 0.79549515, ((0, 128),), jnp.float32),
        "eps_occ": jnp.clip(jax.random.uniform(splits[2], (OCC,), jnp.float32, -2.0, -0.3), -2.0, -0.3),
        "eps_vir": jnp.clip(jax.random.uniform(splits[3], (VIR,), jnp.float32, 0.2, 4.0), 0.2, 4.0),
    }


def reference(t_amps, cholesky, eps_occ, eps_vir):
    blk = OV // (N_ROW * N_COL)
    tmat = t_amps.reshape(OV, N_COL, N_ROW, blk).transpose(0, 2, 1, 3).reshape(OV, OV)
    tl_prod = jnp.dot(tmat, cholesky, precision=lax.Precision.HIGHEST, preferred_element_type=jnp.float32)
    mixed = cholesky + tl_prod
    gaps = (eps_vir[None, :] - eps_occ[:, None]).reshape(OV)
    outer = jnp.dot(mixed, mixed.T, precision=lax.Precision.HIGHEST, preferred_element_type=jnp.float32)
    result = -outer / (gaps[:, None] + gaps[None, :])
    return result.reshape(OV, N_ROW, N_COL, blk).transpose(0, 2, 1, 3).reshape(OV, OV)
```

```python
import functools

import jax
import jax.numpy as jnp
from jax import lax
from jax.experimental import pallas as pl
from jax.experimental.pallas import tpu as pltpu
from jax.sharding import PartitionSpec as P

MESH = pl.DeviceIdType.MESH
BF16 = jnp.bfloat16
F32 = jnp.float32

ORDER = (
    ("M1", 8), ("L1", 0), ("M2", 9), ("M3", 9), ("L2", 0), ("R2", 6), ("R3", 7), ("M0", 7), ("M4", 10), ("X2", 11),
    ("C1", 8), ("L4", 2), ("C2", 9), ("L3", 1), ("C3", 9), ("R1", 4), ("C0", 7), ("C4", 10), ("L0", -2), ("X1", 2),
    ("R0", 2),
)
CHUNK = 256


def split(v):
    hi = v.astype(BF16)
    return hi, (v - hi.astype(F32)).astype(BF16)


def kernel(
    n, t_hbm, l_hbm, out_ref,
    lg, mc, mr, p, ra, rb, rz, tf, t3, l3, m3r, m3c,
    rl_sem, rm_sem, rc_sem, rr_sem, send_sem, local_sem,
):
    blk, kc = rz.shape[1], rz.shape[2]
    depth = tf.shape[1]
    r, c = lax.axis_index("row"), lax.axis_index("col")
    x, zl, core = r // 4, (r // 2) % 2, r % 2
    zh, y = c // 4, c % 4
    xp, xm, x2 = (x + 1) % 4, (x + 3) % 4, (x + 2) % 4
    yp, ym, y2 = (y + 1) % 4, (y + 3) % 4, (y + 2) % 4
    to_xp, to_xm = (xp * 4 + zl * 2 + core, c), (xm * 4 + zl * 2 + core, c)
    to_z, to_core = (x * 4 + (1 - zl) * 2 + core, c), (x * 4 + zl * 2 + 1 - core, c)
    to_yp, to_ym = (r, zh * 4 + yp), (r, zh * 4 + ym)
    to_zh = (r, (1 - zh) * 4 + y)
    own = x * 2 + zl

    load_t = pltpu.make_async_copy(t_hbm, tf, local_sem.at[n])
    for t in range(n):
        pltpu.make_async_copy(l_hbm.at[:, pl.ds(t * kc, kc)], lg.at[t, core, own], local_sem.at[t]).start()
    load_t.start()

    barrier = pltpu.get_barrier_semaphore()
    peers = (to_xp, to_xm, to_z, to_core, to_yp, to_ym, to_zh)
    for peer in peers:
        pl.semaphore_signal(barrier, inc=1, device_id=peer, device_id_type=MESH)
    pl.semaphore_wait(barrier, len(peers))

    def send(src, dst, group, arrive, peer):
        pltpu.make_async_remote_copy(
            src_ref=src, dst_ref=dst, send_sem=send_sem.at[group], recv_sem=arrive, device_id=peer, device_id_type=MESH
        ).start()

    def arrived(ref, sem):
        pltpu.make_async_remote_copy(
            src_ref=ref, dst_ref=ref, send_sem=send_sem.at[0], recv_sem=sem, device_id=to_core, device_id_type=MESH
        ).wait_recv()

    def sent(ref, group):
        pltpu.make_async_remote_copy(
            src_ref=ref, dst_ref=ref, send_sem=send_sem.at[group], recv_sem=rr_sem.at[0, 0], device_id=to_core, device_id_type=MESH
        ).wait_send()

    def over_row(buf, sem, group, t, k):
        def at(slot):
            return buf.at[t, core, slot]

        def out(slot, s, peer):
            send(at(slot), at(slot), group, sem.at[t, s], peer)

        def share(slot):
            send(at(slot), at(slot), group + 1, sem.at[t, 7], to_core)

        def got(slot, s):
            arrived(at(slot), sem.at[t, s])

        near, far = zl, 1 - zl
        if k == 0:
            out(own, 0, to_z)
            out(own, 1, to_xp)
            out(own, 2, to_xm)
            share(own)
        elif k == 1:
            mate = x * 2 + far
            got(mate, 0)
            out(mate, 3, to_xp)
            out(mate, 4, to_xm)
            share(mate)
        elif k == 2:
            got(xm * 2 + near, 1)
            out(xm * 2 + near, 5, to_xp)
            share(xm * 2 + near)
            got(xp * 2 + near, 2)
            share(xp * 2 + near)
        elif k == 3:
            got(xp * 2 + far, 4)
            out(xp * 2 + far, 6, to_xm)
            share(xp * 2 + far)
            got(xm * 2 + far, 3)
            share(xm * 2 + far)
        elif k == 4:
            got(x2 * 2 + near, 5)
            share(x2 * 2 + near)
            got(x2 * 2 + far, 6)
            share(x2 * 2 + far)
        else:
            arrived(buf.at[t, 1 - core], sem.at[t, 7])

    def over_col(t, k):
        def out(slot, s, peer):
            send(mr.at[t, slot], mr.at[t, slot], 5, rc_sem.at[t, s], peer)

        def got(slot, s):
            arrived(mr.at[t, slot], rc_sem.at[t, s])

        near, far = zh * 4, (1 - zh) * 4
        if k == 0:
            out(c, 0, to_zh)
            out(c, 1, to_yp)
            out(c, 2, to_ym)
        elif k == 1:
            got(far + y, 0)
            out(far + y, 3, to_yp)
            out(far + y, 4, to_ym)
        elif k == 2:
            got(near + ym, 1)
            out(near + ym, 5, to_yp)
            got(near + yp, 2)
        elif k == 3:
            got(far + yp, 4)
            out(far + yp, 6, to_ym)
            got(far + ym, 3)
        else:
            got(near + y2, 5)
            got(far + y2, 6)

    def part(t, col):
        return p.at[t, pl.ds(pl.multiple_of(col * blk, blk), blk)]

    def sums(t, k):
        def out(src, dst, s, peer):
            send(src, dst, 4, rr_sem.at[t, s], peer)

        if k == 0:
            out(part(t, y2), ra.at[t, 0], 0, to_yp)
            out(part(t, 4 + y2), ra.at[t, 1], 1, to_ym)
            out(part(t, 4 + yp), rb.at[t, 0, 1], 3, to_yp)
            out(part(t, ym), rb.at[t, 1, 0], 4, to_ym)
        elif k == 1:
            arrived(ra.at[t, 0], rr_sem.at[t, 0])
            plus = part(t, yp)
            plus[...] = plus[...] + ra[t, 0]
            out(plus, rb.at[t, 0, 0], 2, to_yp)
            arrived(ra.at[t, 1], rr_sem.at[t, 1])
            minus = part(t, 4 + ym)
            minus[...] = minus[...] + ra[t, 1]
            out(minus, rb.at[t, 1, 1], 5, to_ym)
        elif k == 2:
            arrived(rb.at[t, 0, 0], rr_sem.at[t, 2])
            arrived(rb.at[t, 0, 1], rr_sem.at[t, 3])
            arrived(rb.at[t, 1, 0], rr_sem.at[t, 4])
            arrived(rb.at[t, 1, 1], rr_sem.at[t, 5])
            other = part(t, (1 - zh) * 4 + y)
            other[...] = other[...] + rb[t, 0, 1 - zh] + rb[t, 1, 1 - zh]
            out(other, rz.at[t], 6, to_zh)
        else:
            arrived(rz.at[t], rr_sem.at[t, 6])
            m = lg[t, core, own] + (part(t, c)[...] + rb[t, 0, zh] + rb[t, 1, zh] + rz[t])
            mc[t, core, own] = m
            mr[t, c] = m

    def rows_of(buf, t):
        for block in range(16):
            yield pl.ds(block * blk, blk), buf[t, block % 2, block // 2]

    def product_tl(t):
        over_row(lg, rl_sem, 0, t, 5)
        for rows, v in rows_of(lg, t):
            hi, lo = split(v)
            l3[rows, :] = hi
            l3[pl.ds(depth + rows.start, blk), :] = lo
            l3[pl.ds(2 * depth + rows.start, blk), :] = hi
        p[t] = jnp.dot(t3[...], l3[...], preferred_element_type=F32)

    def product_mm(t):
        over_row(mc, rm_sem, 2, t, 5)
        for block in range(8):
            hi, lo = split(mr[t, block])
            rows = pl.ds(block * blk, blk)
            m3r[rows, :kc] = hi
            m3r[rows, kc : 2 * kc] = hi
            m3r[rows, 2 * kc :] = lo
        for rows, v in rows_of(mc, t):
            hi, lo = split(v)
            m3c[rows, :kc] = hi
            m3c[rows, kc : 2 * kc] = lo
            m3c[rows, 2 * kc :] = hi
        out_ref[...] += lax.dot_general(
            m3r[...], m3c[...], (((1,), (1,)), ((), ())), preferred_element_type=F32
        )

    def prepare_t():
        load_t.wait()
        hi, lo = split(tf[...])
        t3[:, :depth] = hi
        t3[:, depth : 2 * depth] = hi
        t3[:, 2 * depth :] = lo
        out_ref[...] = jnp.zeros_like(out_ref)

    def stage(name, t):
        kind, k = name[0], int(name[1])
        if name == "L0":
            pltpu.make_async_copy(l_hbm.at[:, pl.ds(0, kc)], lg.at[t, core, own], local_sem.at[t]).wait()
        if kind == "L":
            over_row(lg, rl_sem, 0, t, k)
        elif kind == "M":
            over_row(mc, rm_sem, 2, t, k)
        elif kind == "C":
            over_col(t, k)
        elif kind == "R":
            sums(t, k)
        elif name == "X1":
            product_tl(t)
        else:
            product_mm(t)

    first = min(d for _, d in ORDER)
    last = n + max(d for _, d in ORDER)

    def step(i, carry):
        for name, delay in ORDER:
            t = i + (first - delay)

            @pl.when((t >= 0) & (t < n))
            def _(name=name, t=t):
                stage(name, t)

            if name == "L0":

                @pl.when(t == 0)
                def _():
                    prepare_t()

        return carry

    lax.fori_loop(0, last - first, step, 0)

    for buf, group in ((lg, 0), (mc, 2)):
        sent(buf.at[:, 0, pl.ds(0, 7)], group)
        sent(buf.at[:, 0], group + 1)
    sent(mr.at[:, pl.ds(0, 7)], 4)
    sent(mr.at[:, pl.ds(0, 7)], 5)


def products(t_amps, cholesky):
    rows, depth = t_amps.shape
    blk, chol = cholesky.shape
    kc = CHUNK
    n = chol // kc
    vmem = lambda shape, dtype=F32: pltpu.VMEM(shape, dtype)
    dma = pltpu.SemaphoreType.DMA
    return pl.pallas_call(
        functools.partial(kernel, n),
        out_shape=jax.ShapeDtypeStruct((rows, depth), F32),
        in_specs=[pl.BlockSpec(memory_space=pl.ANY)] * 2,
        out_specs=pl.BlockSpec(memory_space=pltpu.VMEM),
        scratch_shapes=[
            vmem((n, 2, 8, blk, kc)),
            vmem((n, 2, 8, blk, kc)),
            vmem((n, 8, blk, kc)),
            vmem((n, rows, kc)),
            vmem((n, 2, blk, kc)),
            vmem((n, 2, 2, blk, kc)),
            vmem((n, blk, kc)),
            vmem((rows, depth)),
            vmem((rows, 3 * depth), BF16),
            vmem((3 * depth, kc), BF16),
            vmem((rows, 3 * kc), BF16),
            vmem((depth, 3 * kc), BF16),
            dma((n, 8)),
            dma((n, 8)),
            dma((n, 7)),
            dma((n, 7)),
            dma((6,)),
            dma((n + 1,)),
        ],
        compiler_params=pltpu.CompilerParams(collective_id=0, has_side_effects=True, vmem_limit_bytes=56 * 2**20),
    )(t_amps, cholesky)


def shards(t_amps, cholesky, eps_occ, eps_vir):
    rows_blk, width = t_amps.shape
    nrow = lax.axis_size("row")
    ncol = lax.axis_size("col")
    blk = width // nrow
    outer = products(t_amps, cholesky)
    gaps = (eps_vir[None, :] - eps_occ[:, None]).reshape(nrow * rows_blk)
    row_gap = lax.dynamic_slice_in_dim(gaps, lax.axis_index("row") * rows_blk, rows_blk, 0)
    col_gap = lax.dynamic_slice_in_dim(gaps.reshape(nrow, ncol, blk), lax.axis_index("col"), 1, 1).reshape(nrow * blk)
    return -outer / (row_gap[:, None] + col_gap[None, :])


def solution(mesh):
    in_specs = (P("row", "col"), P(("row", "col"), None), P(), P())
    out_specs = P("row", "col")
    return jax.shard_map(shards, mesh=mesh, in_specs=in_specs, out_specs=out_specs, check_vma=False)
```

```python
import functools

import jax
import jax.numpy as jnp
from jax import lax
from jax.experimental import pallas as pl
from jax.experimental.pallas import tpu as pltpu
from jax.sharding import PartitionSpec as P

MESH = pl.DeviceIdType.MESH
BF16 = jnp.bfloat16
F32 = jnp.float32

ORDER = (
    ("X2", 16), ("M5", 13), ("R4", 9), ("M0", 9), ("L1", 2), ("X1", 5), ("R0", 5), ("C4", 14), ("R1", 6), ("C3", 13),
    ("L3", 3), ("M1", 10), ("C2", 12), ("R2", 6), ("M4", 12), ("C1", 11), ("L2", 2), ("L4", 4), ("M2", 10), ("M3", 11),
    ("C5", 15), ("L0", 0), ("L5", 4), ("C0", 9), ("R3", 7),
)
CHUNK = 256
BY_Z = {"L": (), "M": (), "C": (0, 3), "R": ()}


def split(v):
    hi = v.astype(BF16)
    return hi, (v - hi.astype(F32)).astype(BF16)


def kernel(
    n, t_hbm, l_hbm, occ_hbm, vir_hbm, out_ref,
    lg, mc, mr, p, ra, rb, rz, tf, t3, l3, m3r, m3c, inv, occ, vir,
    rl_sem, rm_sem, rc_sem, rr_sem, send_sem, local_sem,
):
    blk, kc = rz.shape[2], rz.shape[3]
    depth = tf.shape[1]
    r, c = lax.axis_index("row"), lax.axis_index("col")
    x, zl, core = r // 4, (r // 2) % 2, r % 2
    zh, y = c // 4, c % 4
    xp, xm, x2 = (x + 1) % 4, (x + 3) % 4, (x + 2) % 4
    yp, ym, y2 = (y + 1) % 4, (y + 3) % 4, (y + 2) % 4
    to_xp, to_xm = (xp * 4 + zl * 2 + core, c), (xm * 4 + zl * 2 + core, c)
    to_z, to_core = (x * 4 + (1 - zl) * 2 + core, c), (x * 4 + zl * 2 + 1 - core, c)
    to_yp, to_ym = (r, zh * 4 + yp), (r, zh * 4 + ym)
    to_zh = (r, (1 - zh) * 4 + y)
    own = x * 2 + zl

    half = blk // 2

    barrier = pltpu.get_barrier_semaphore()
    peers = (to_xp, to_xm, to_z, to_core, to_yp, to_ym, to_zh)
    for peer in peers:
        pl.semaphore_signal(barrier, inc=1, device_id=peer, device_id_type=MESH)
    load_occ = pltpu.make_async_copy(occ_hbm, occ, local_sem.at[n + 1])
    load_vir = pltpu.make_async_copy(vir_hbm, vir, local_sem.at[n + 2])
    load_t = pltpu.make_async_copy(t_hbm, tf, local_sem.at[n])
    load_occ.start()
    load_vir.start()
    for t in range(n):
        pltpu.make_async_copy(l_hbm.at[:, pl.ds(t * kc, kc)], lg.at[t, core, own], local_sem.at[t]).start()
    load_t.start()

    load_occ.wait()
    load_vir.wait()
    lanes = 2 * blk
    lane = lax.broadcasted_iota(jnp.int32, (1, lanes), 1)
    low, high = vir[pl.ds(c // 2, 1), :], vir[pl.ds(4 + c // 2, 1), :]
    even = jnp.where(lane < blk, low, pltpu.roll(high, blk, 1))
    odd = jnp.where(lane < blk, pltpu.roll(low, blk, 1), high)
    col_vir = jnp.where(c % 2 == 0, even, odd)
    for a in range(4):
        row_vir = jnp.broadcast_to(vir[pl.ds((r % 2) * 4 + a, 1), :], (lanes, lanes)).T
        row_gap = row_vir - occ[r // 2]
        for g in range(8):
            col_gap = col_vir - occ[g]
            inv[pl.ds(a * lanes, lanes), pl.ds(g * lanes, lanes)] = -1.0 / (row_gap + col_gap)
    out_ref[...] = jnp.zeros_like(out_ref)

    pl.semaphore_wait(barrier, len(peers))

    def send(src, dst, group, arrive, peer):
        pltpu.make_async_remote_copy(
            src_ref=src, dst_ref=dst, send_sem=send_sem.at[group], recv_sem=arrive, device_id=peer, device_id_type=MESH
        ).start()

    def arrived(ref, sem):
        pltpu.make_async_remote_copy(
            src_ref=ref, dst_ref=ref, send_sem=send_sem.at[0], recv_sem=sem, device_id=to_core, device_id_type=MESH
        ).wait_recv()

    def sent(ref, group):
        pltpu.make_async_remote_copy(
            src_ref=ref, dst_ref=ref, send_sem=send_sem.at[group], recv_sem=rr_sem.at[0, 0], device_id=to_core, device_id_type=MESH
        ).wait_send()

    def over_row(buf, sem, group, t, k, by_z=False):
        def at(slot):
            return buf.at[t, core, slot]

        def out(slot, s, peer):
            send(at(slot), at(slot), group, sem.at[t, s], peer)

        def share(slot):
            send(at(slot), at(slot), group + 1, sem.at[t, 7], to_core)

        def got(slot, s):
            arrived(at(slot), sem.at[t, s])

        def pass_on(slot, first, s, peer):
            ref = at(slot).at[pl.ds(first, half)]
            send(ref, ref, group, sem.at[t, s], peer)

        near, far = zl, 1 - zl
        if by_z and k == 0:
            out(own, 1, to_xp)
            out(own, 2, to_xm)
            out(own, 0, to_z)
            share(own)
        elif by_z and k == 1:
            got(x * 2 + far, 0)
            share(x * 2 + far)
        elif by_z and k == 2:
            got(xm * 2 + near, 1)
            pass_on(xm * 2 + near, 0, 5, to_xp)
            out(xm * 2 + near, 3, to_z)
            share(xm * 2 + near)
        elif by_z and k == 3:
            got(xp * 2 + near, 2)
            pass_on(xp * 2 + near, half, 6, to_xm)
            out(xp * 2 + near, 4, to_z)
            share(xp * 2 + near)
        elif by_z and k == 4:
            arrived(at(x2 * 2 + near).at[pl.ds(0, half)], sem.at[t, 5])
            arrived(at(x2 * 2 + near).at[pl.ds(half, half)], sem.at[t, 6])
            out(x2 * 2 + near, 8, to_z)
            share(x2 * 2 + near)
        elif by_z:
            for slot, s in ((xm, 3), (xp, 4), (x2, 8)):
                got(slot * 2 + far, s)
                share(slot * 2 + far)
        elif k == 0:
            out(own, 0, to_z)
            out(own, 1, to_xp)
            out(own, 2, to_xm)
            share(own)
        elif k == 1:
            mate = x * 2 + far
            got(mate, 0)
            out(mate, 3, to_xp)
            out(mate, 4, to_xm)
            share(mate)
        elif k == 2:
            got(xm * 2 + near, 1)
            out(xm * 2 + near, 5, to_xp)
            share(xm * 2 + near)
        elif k == 3:
            got(xp * 2 + far, 4)
            out(xp * 2 + far, 6, to_xm)
            share(xp * 2 + far)
        elif k == 4:
            got(xp * 2 + near, 2)
            share(xp * 2 + near)
            got(xm * 2 + far, 3)
            share(xm * 2 + far)
        else:
            got(x2 * 2 + near, 5)
            share(x2 * 2 + near)
            got(x2 * 2 + far, 6)
            share(x2 * 2 + far)

    def over_col(t, k, by_z=False):
        def out(slot, s, peer):
            send(mr.at[t, slot], mr.at[t, slot], 5, rc_sem.at[t, s], peer)

        def got(slot, s):
            arrived(mr.at[t, slot], rc_sem.at[t, s])

        def pass_on(slot, first, s, peer):
            ref = mr.at[t, slot, pl.ds(first, half)]
            send(ref, ref, 5, rc_sem.at[t, s], peer)

        near, far = zh * 4, (1 - zh) * 4
        if by_z and k == 0:
            out(c, 1, to_yp)
            out(c, 2, to_ym)
            out(c, 0, to_zh)
        elif by_z and k == 1:
            got(far + y, 0)
        elif by_z and k == 2:
            got(near + ym, 1)
            pass_on(near + ym, 0, 5, to_yp)
            out(near + ym, 3, to_zh)
        elif by_z and k == 3:
            got(near + yp, 2)
            pass_on(near + yp, half, 6, to_ym)
            out(near + yp, 4, to_zh)
        elif by_z and k == 4:
            arrived(mr.at[t, near + y2, pl.ds(0, half)], rc_sem.at[t, 5])
            arrived(mr.at[t, near + y2, pl.ds(half, half)], rc_sem.at[t, 6])
            out(near + y2, 7, to_zh)
        elif by_z:
            for slot, s in ((ym, 3), (yp, 4), (y2, 7)):
                got(far + slot, s)
        elif k == 0:
            out(c, 0, to_zh)
            out(c, 1, to_yp)
            out(c, 2, to_ym)
        elif k == 1:
            got(far + y, 0)
            out(far + y, 3, to_yp)
            out(far + y, 4, to_ym)
        elif k == 2:
            got(near + ym, 1)
            out(near + ym, 5, to_yp)
        elif k == 3:
            got(far + yp, 4)
            out(far + yp, 6, to_ym)
        elif k == 4:
            got(near + yp, 2)
            got(far + ym, 3)
        else:
            got(near + y2, 5)
            got(far + y2, 6)

    def part(t, col, first=0, rows=blk):
        return p.at[t, pl.ds(pl.multiple_of(col * blk + first, half), rows)]

    def block(t, k):
        return rb.at[t, pl.ds(pl.multiple_of(k * blk, blk), blk)]

    def add(ref, *others):
        total = ref[...]
        for other in others:
            total = total + other[...]
        ref[...] = total

    def sums(t, k, by_z=False):
        def out(src, dst, s, peer):
            send(src, dst, 4, rr_sem.at[t, s], peer)

        def got(ref, s):
            arrived(ref, rr_sem.at[t, s])

        near, far = zh * 4, (1 - zh) * 4
        if by_z and k == 0:
            out(part(t, far, 0, 4 * blk), rb.at[t], 6, to_zh)
        elif by_z and k == 1:
            got(rb.at[t], 6)
            add(part(t, near, 0, 4 * blk), rb.at[t])
            out(part(t, near + y2, 0, half), ra.at[t, 0, pl.ds(0, half)], 0, to_yp)
            out(part(t, near + y2, half, half), ra.at[t, 1, pl.ds(half, half)], 1, to_ym)
        elif by_z and k == 2:
            plus, minus = ra.at[t, 0, pl.ds(0, half)], ra.at[t, 1, pl.ds(half, half)]
            got(plus, 0)
            add(part(t, near + yp, 0, half), plus)
            out(part(t, near + yp), rz.at[t, 0], 2, to_yp)
            got(minus, 1)
            add(part(t, near + ym, half, half), minus)
            out(part(t, near + ym), rz.at[t, 1], 5, to_ym)
        elif by_z and k == 3:
            got(rz.at[t, 0], 2)
            got(rz.at[t, 1], 5)
            finish(t, rz.at[t, 0], rz.at[t, 1])
        elif by_z:
            pass
        elif k == 0:
            out(part(t, y2), ra.at[t, 0], 0, to_yp)
            out(part(t, 4 + y2), ra.at[t, 1], 1, to_ym)
            out(part(t, 4 + yp), block(t, 1), 3, to_yp)
            out(part(t, ym), block(t, 2), 4, to_ym)
        elif k == 1:
            got(ra.at[t, 0], 0)
            add(part(t, yp), ra.at[t, 0])
            out(part(t, yp), block(t, 0), 2, to_yp)
        elif k == 2:
            got(ra.at[t, 1], 1)
            add(part(t, 4 + ym), ra.at[t, 1])
            out(part(t, 4 + ym), block(t, 3), 5, to_ym)
        elif k == 3:
            for i in range(4):
                got(block(t, i), 2 + i)
            other = part(t, far + y)
            add(other, block(t, 1 - zh), block(t, 3 - zh))
            out(other, rz.at[t, 0], 6, to_zh)
        else:
            got(rz.at[t, 0], 6)
            finish(t, block(t, zh), block(t, 2 + zh), rz.at[t, 0])

    def finish(t, *others):
        add(part(t, c), *others)
        m = lg[t, core, own] + part(t, c)[...]
        mc[t, core, own] = m
        mr[t, c] = m

    def rows_of(buf, t):
        for i in range(16):
            yield pl.ds(i * blk, blk), buf[t, i % 2, i // 2]

    def product_tl(t):
        arrived(lg.at[t, 1 - core], rl_sem.at[t, 7])
        for rows, v in rows_of(lg, t):
            hi, lo = split(v)
            l3[rows, :] = hi
            l3[pl.ds(depth + rows.start, blk), :] = lo
            l3[pl.ds(2 * depth + rows.start, blk), :] = hi
        p[t] = jnp.dot(t3[...], l3[...], preferred_element_type=F32)

    def product_mm(t):
        arrived(mc.at[t, 1 - core], rm_sem.at[t, 7])
        for i in range(8):
            hi, lo = split(mr[t, i])
            rows = pl.ds(i * blk, blk)
            m3r[rows, :kc] = hi
            m3r[rows, kc : 2 * kc] = hi
            m3r[rows, 2 * kc :] = lo
        for rows, v in rows_of(mc, t):
            hi, lo = split(v)
            m3c[rows, :kc] = hi
            m3c[rows, kc : 2 * kc] = lo
            m3c[rows, 2 * kc :] = hi
        out_ref[...] += lax.dot_general(
            m3r[...], m3c[...], (((1,), (1,)), ((), ())), preferred_element_type=F32
        )

        @pl.when(t == n - 1)
        def _():
            out_ref[...] = out_ref[...] * inv[...]

    def prepare_t():
        load_t.wait()
        hi, lo = split(tf[...])
        t3[:, :depth] = hi
        t3[:, depth : 2 * depth] = hi
        t3[:, 2 * depth :] = lo

    move = {
        "L": functools.partial(over_row, lg, rl_sem, 0),
        "M": functools.partial(over_row, mc, rm_sem, 2),
        "C": over_col,
        "R": sums,
    }

    def stage(name, t):
        kind, k = name[0], int(name[1])
        if name == "L0":
            pltpu.make_async_copy(l_hbm.at[:, pl.ds(0, kc)], lg.at[t, core, own], local_sem.at[t]).wait()
        if kind in move:
            if not BY_Z[kind]:
                move[kind](t, k)
            else:
                z = functools.reduce(jnp.logical_or, [t == i for i in BY_Z[kind]])
                pl.when(z)(lambda: move[kind](t, k, True))
                pl.when(jnp.logical_not(z))(lambda: move[kind](t, k))
        elif name == "X1":
            product_tl(t)
        else:
            product_mm(t)

    first = min(d for _, d in ORDER)
    last = n + max(d for _, d in ORDER)

    def step(i, carry):
        for name, delay in ORDER:
            t = i + (first - delay)

            @pl.when((t >= 0) & (t < n))
            def _(name=name, t=t):
                stage(name, t)

            if name == "L0":

                @pl.when(t == 0)
                def _():
                    prepare_t()

        return carry

    lax.fori_loop(0, last - first, step, 0)

    for buf, group in ((lg, 0), (mc, 2)):
        sent(buf.at[:, 0, pl.ds(0, 7)], group)
        sent(buf.at[:, 0], group + 1)
    sent(mr.at[:, pl.ds(0, 7)], 4)
    sent(mr.at[:, pl.ds(0, 7)], 5)


def shards(t_amps, cholesky, eps_occ, eps_vir):
    eps_vir = eps_vir.reshape(8, -1)
    rows, depth = t_amps.shape
    blk, chol = cholesky.shape
    kc = CHUNK
    n = chol // kc
    vmem = lambda shape, dtype=F32: pltpu.VMEM(shape, dtype)
    dma = pltpu.SemaphoreType.DMA
    return pl.pallas_call(
        functools.partial(kernel, n),
        out_shape=jax.ShapeDtypeStruct((rows, depth), F32),
        in_specs=[pl.BlockSpec(memory_space=pltpu.MemorySpace.HBM)] * 4,
        out_specs=pl.BlockSpec(memory_space=pltpu.VMEM),
        scratch_shapes=[
            vmem((n, 2, 8, blk, kc)),
            vmem((n, 2, 8, blk, kc)),
            vmem((n, 8, blk, kc)),
            vmem((n, rows, kc)),
            vmem((n, 2, blk, kc)),
            vmem((n, 4 * blk, kc)),
            vmem((n, 2, blk, kc)),
            vmem((rows, depth)),
            vmem((rows, 3 * depth), BF16),
            vmem((3 * depth, kc), BF16),
            vmem((rows, 3 * kc), BF16),
            vmem((depth, 3 * kc), BF16),
            vmem((rows, depth)),
            pltpu.SMEM(eps_occ.shape, F32),
            vmem(eps_vir.shape),
            dma((n, 9)),
            dma((n, 9)),
            dma((n, 8)),
            dma((n, 7)),
            dma((6,)),
            dma((n + 3,)),
        ],
        compiler_params=pltpu.CompilerParams(collective_id=0, has_side_effects=True, vmem_limit_bytes=46 * 2**20),
    )(*(pltpu.with_memory_space_constraint(v, pltpu.MemorySpace.HBM) for v in (t_amps, cholesky, eps_occ, eps_vir)))


def solution(mesh):
    in_specs = (P("row", "col"), P(("row", "col"), None), P(), P())
    out_specs = P("row", "col")
    return jax.shard_map(shards, mesh=mesh, in_specs=in_specs, out_specs=out_specs, check_vma=False)
```

```python
import functools

import jax
import jax.numpy as jnp
from jax import lax
from jax.experimental import pallas as pl
from jax.experimental.pallas import tpu as pltpu
from jax.sharding import PartitionSpec as P

MESH = pl.DeviceIdType.MESH
BF16 = jnp.bfloat16
F32 = jnp.float32

SEQ = (
    ("L0", 1), ("L0", 6), ("L0", 0), ("L1", 1), ("L0", 7), ("L2", 6), ("L1", 6), ("L2", 1), ("L3", 6), ("L1", 0), ("L3", 1), ("L0", 4), ("L2", 0), ("L1", 7), ("L4", 6), ("L2", 7), ("L3", 0), ("L4", 1), ("L5", 1),
    ("L3", 7), ("L4", 0), ("L1", 4), ("L0", 2), ("L0", 3), ("L5", 6), ("X1", 1), ("R0", 1), ("L5", 0), ("L2", 4), ("L4", 7), ("X1", 6), ("R0", 6), ("L1", 2), ("X1", 0), ("R0", 0), ("L3", 4), ("L2", 2), ("L1", 3),
    ("L5", 7), ("R1", 1), ("L4", 4), ("R2", 1), ("L3", 2), ("L0", 5), ("X1", 7), ("R0", 7), ("R1", 6), ("L4", 2), ("R2", 6), ("L5", 4), ("R1", 0), ("L2", 3), ("R2", 0), ("L3", 3), ("L5", 2), ("X1", 4), ("R0", 4),
    ("L1", 5), ("X1", 2), ("R3", 6), ("L4", 3), ("R0", 2), ("L5", 3), ("R3", 0), ("R1", 4), ("L2", 5), ("R3", 1), ("L3", 5), ("R2", 4), ("X1", 3), ("R1", 7), ("R0", 3), ("R4", 6), ("M0", 6), ("L4", 5), ("R1", 2),
    ("R2", 2), ("R4", 0), ("M0", 0), ("R4", 1), ("C0", 6), ("L5", 5), ("R3", 4), ("R2", 7), ("M0", 1), ("X1", 5), ("R1", 3), ("M1", 6), ("R2", 3), ("R0", 5), ("C0", 1), ("M2", 0), ("M2", 6), ("M1", 0), ("R3", 2),
    ("C0", 0), ("R4", 4), ("M0", 4), ("M1", 1), ("M2", 1), ("R3", 7), ("M3", 6), ("R3", 3), ("M4", 6), ("R4", 7), ("M0", 7), ("R1", 5), ("R2", 5), ("C0", 4), ("C0", 7), ("M3", 0), ("C2", 6), ("R4", 2), ("M1", 4),
    ("M3", 1), ("M0", 2), ("C1", 6), ("M4", 0), ("R4", 3), ("R3", 5), ("C0", 3), ("M0", 3), ("C1", 1), ("M1", 7), ("C1", 7), ("M2", 4), ("C0", 2), ("C3", 6), ("C1", 4), ("M3", 4), ("M1", 2), ("R4", 5), ("M0", 5),
    ("C0", 5), ("M2", 7), ("C1", 3), ("C2", 3), ("M4", 1), ("M4", 4), ("C2", 7), ("M2", 2), ("C3", 7), ("M1", 3), ("C3", 3), ("C2", 1), ("C4", 6), ("M5", 6), ("M5", 4), ("C1", 0), ("C3", 1), ("M3", 7), ("M1", 5),
    ("M2", 3), ("C2", 4), ("M5", 1), ("C3", 4), ("M3", 2), ("C5", 6), ("C1", 2), ("M4", 7), ("C4", 7), ("M4", 2), ("C4", 3), ("C2", 2), ("C1", 5), ("C2", 0), ("M3", 3), ("X2", 6), ("M5", 0), ("C4", 4), ("C3", 2),
    ("M5", 7), ("M2", 5), ("C3", 0), ("M3", 5), ("M4", 5), ("M4", 3), ("C4", 1), ("C5", 1), ("X2", 1), ("C5", 4), ("C2", 5), ("X2", 4), ("C3", 5), ("M5", 2), ("C5", 7), ("C4", 2), ("M5", 3), ("X2", 7), ("C5", 3),
    ("M5", 5), ("C4", 5), ("C4", 0), ("C5", 0), ("X2", 0), ("X2", 3), ("C5", 5), ("X2", 5), ("C5", 2), ("X2", 2),
)
WIDTHS = (256, 256, 256, 256, 256, 256, 256, 256)
BY_Z = {"L": (6, 7), "M": (), "C": (2, 3, 7), "R": (7,)}


def split(v):
    hi = v.astype(BF16)
    return hi, (v - hi.astype(F32)).astype(BF16)


def kernel(
    t_hbm, l_hbm, occ_hbm, vir_hbm, out_ref,
    wide, slim, tf, t3, l3, m3r, m3c, inv, occ, vir,
    rl_sem, rm_sem, rc_sem, rr_sem, send_sem, local_sem,
):
    n, blk = len(WIDTHS), l_hbm.shape[0]
    full = max(WIDTHS)
    counts = [0, 0]
    places = []
    for width in WIDTHS:
        kind = int(width < full)
        places.append(((wide, slim)[kind], counts[kind]))
        counts[kind] += 1
    thin = [int(width < full) for width in WIDTHS]
    lg, mc, mr, p, ra, rb, rz = ([bufs[i].at[j] for bufs, j in places] for i in range(7))
    depth = tf.shape[1]
    r, c = lax.axis_index("row"), lax.axis_index("col")
    x, zl, core = r // 4, (r // 2) % 2, r % 2
    zh, y = c // 4, c % 4
    xp, xm, x2 = (x + 1) % 4, (x + 3) % 4, (x + 2) % 4
    yp, ym, y2 = (y + 1) % 4, (y + 3) % 4, (y + 2) % 4
    to_xp, to_xm = (xp * 4 + zl * 2 + core, c), (xm * 4 + zl * 2 + core, c)
    to_z, to_core = (x * 4 + (1 - zl) * 2 + core, c), (x * 4 + zl * 2 + 1 - core, c)
    to_yp, to_ym = (r, zh * 4 + yp), (r, zh * 4 + ym)
    to_zh = (r, (1 - zh) * 4 + y)
    own = x * 2 + zl

    half = blk // 2

    barrier = pltpu.get_barrier_semaphore()
    peers = (to_xp, to_xm, to_z, to_core, to_yp, to_ym, to_zh)
    for peer in peers:
        pl.semaphore_signal(barrier, inc=1, device_id=peer, device_id_type=MESH)
    load_occ = pltpu.make_async_copy(occ_hbm, occ, local_sem.at[n + 1])
    load_vir = pltpu.make_async_copy(vir_hbm, vir, local_sem.at[n + 2])
    load_t = pltpu.make_async_copy(t_hbm, tf, local_sem.at[n])
    load_occ.start()
    load_vir.start()
    for t in range(n):
        pltpu.make_async_copy(l_hbm.at[:, pl.ds(sum(WIDTHS[:t]), WIDTHS[t])], lg[t].at[core, own], local_sem.at[t]).start()
    load_t.start()

    load_occ.wait()
    load_vir.wait()
    lanes = 2 * blk
    lane = lax.broadcasted_iota(jnp.int32, (1, lanes), 1)
    low, high = vir[pl.ds(c // 2, 1), :], vir[pl.ds(4 + c // 2, 1), :]
    even = jnp.where(lane < blk, low, pltpu.roll(high, blk, 1))
    odd = jnp.where(lane < blk, pltpu.roll(low, blk, 1), high)
    col_vir = jnp.where(c % 2 == 0, even, odd)
    for a in range(4):
        row_vir = jnp.broadcast_to(vir[pl.ds((r % 2) * 4 + a, 1), :], (lanes, lanes)).T
        row_gap = row_vir - occ[r // 2]
        for g in range(8):
            col_gap = col_vir - occ[g]
            inv[pl.ds(a * lanes, lanes), pl.ds(g * lanes, lanes)] = -1.0 / (row_gap + col_gap)
    out_ref[...] = jnp.zeros_like(out_ref)

    pl.semaphore_wait(barrier, len(peers))

    def send(src, dst, group, arrive, peer):
        pltpu.make_async_remote_copy(
            src_ref=src, dst_ref=dst, send_sem=send_sem.at[group], recv_sem=arrive, device_id=peer, device_id_type=MESH
        ).start()

    def arrived(ref, sem):
        pltpu.make_async_remote_copy(
            src_ref=ref, dst_ref=ref, send_sem=send_sem.at[0], recv_sem=sem, device_id=to_core, device_id_type=MESH
        ).wait_recv()

    def sent(ref, group):
        pltpu.make_async_remote_copy(
            src_ref=ref, dst_ref=ref, send_sem=send_sem.at[group], recv_sem=rr_sem.at[0, 0], device_id=to_core, device_id_type=MESH
        ).wait_send()

    def over_row(buf, sem, group, t, k, by_z=False):
        def at(slot):
            return buf[t].at[core, slot]

        def out(slot, s, peer):
            send(at(slot), at(slot), group + 6 * thin[t], sem.at[t, s], peer)

        def share(slot):
            send(at(slot), at(slot), group + 1 + 6 * thin[t], sem.at[t, 7], to_core)

        def got(slot, s):
            arrived(at(slot), sem.at[t, s])

        def pass_on(slot, first, s, peer):
            ref = at(slot).at[pl.ds(first, half)]
            send(ref, ref, group + 6 * thin[t], sem.at[t, s], peer)

        near, far = zl, 1 - zl
        if by_z and k == 0:
            out(own, 1, to_xp)
            out(own, 2, to_xm)
            out(own, 0, to_z)
            share(own)
        elif by_z and k == 1:
            got(x * 2 + far, 0)
            share(x * 2 + far)
        elif by_z and k == 2:
            got(xm * 2 + near, 1)
            pass_on(xm * 2 + near, 0, 5, to_xp)
            out(xm * 2 + near, 3, to_z)
            share(xm * 2 + near)
        elif by_z and k == 3:
            got(xp * 2 + near, 2)
            pass_on(xp * 2 + near, half, 6, to_xm)
            out(xp * 2 + near, 4, to_z)
            share(xp * 2 + near)
        elif by_z and k == 4:
            arrived(at(x2 * 2 + near).at[pl.ds(0, half)], sem.at[t, 5])
            arrived(at(x2 * 2 + near).at[pl.ds(half, half)], sem.at[t, 6])
            out(x2 * 2 + near, 8, to_z)
            share(x2 * 2 + near)
        elif by_z:
            for slot, s in ((xm, 3), (xp, 4), (x2, 8)):
                got(slot * 2 + far, s)
                share(slot * 2 + far)
        elif k == 0:
            out(own, 0, to_z)
            out(own, 1, to_xp)
            out(own, 2, to_xm)
            share(own)
        elif k == 1:
            mate = x * 2 + far
            got(mate, 0)
            out(mate, 3, to_xp)
            out(mate, 4, to_xm)
            share(mate)
        elif k == 2:
            got(xm * 2 + near, 1)
            out(xm * 2 + near, 5, to_xp)
            share(xm * 2 + near)
        elif k == 3:
            got(xp * 2 + far, 4)
            out(xp * 2 + far, 6, to_xm)
            share(xp * 2 + far)
        elif k == 4:
            got(xp * 2 + near, 2)
            share(xp * 2 + near)
            got(xm * 2 + far, 3)
            share(xm * 2 + far)
        else:
            got(x2 * 2 + near, 5)
            share(x2 * 2 + near)
            got(x2 * 2 + far, 6)
            share(x2 * 2 + far)

    def over_col(t, k, by_z=False):
        def out(slot, s, peer):
            send(mr[t].at[slot], mr[t].at[slot], 5 + 6 * thin[t], rc_sem.at[t, s], peer)

        def got(slot, s):
            arrived(mr[t].at[slot], rc_sem.at[t, s])

        def pass_on(slot, first, s, peer):
            ref = mr[t].at[slot, pl.ds(first, half)]
            send(ref, ref, 5 + 6 * thin[t], rc_sem.at[t, s], peer)

        near, far = zh * 4, (1 - zh) * 4
        if by_z and k == 0:
            out(c, 1, to_yp)
            out(c, 2, to_ym)
            out(c, 0, to_zh)
        elif by_z and k == 1:
            got(far + y, 0)
        elif by_z and k == 2:
            got(near + ym, 1)
            pass_on(near + ym, 0, 5, to_yp)
            out(near + ym, 3, to_zh)
        elif by_z and k == 3:
            got(near + yp, 2)
            pass_on(near + yp, half, 6, to_ym)
            out(near + yp, 4, to_zh)
        elif by_z and k == 4:
            arrived(mr[t].at[near + y2, pl.ds(0, half)], rc_sem.at[t, 5])
            arrived(mr[t].at[near + y2, pl.ds(half, half)], rc_sem.at[t, 6])
            out(near + y2, 7, to_zh)
        elif by_z:
            for slot, s in ((ym, 3), (yp, 4), (y2, 7)):
                got(far + slot, s)
        elif k == 0:
            out(c, 0, to_zh)
            out(c, 1, to_yp)
            out(c, 2, to_ym)
        elif k == 1:
            got(far + y, 0)
            out(far + y, 3, to_yp)
            out(far + y, 4, to_ym)
        elif k == 2:
            got(near + ym, 1)
            out(near + ym, 5, to_yp)
        elif k == 3:
            got(far + yp, 4)
            out(far + yp, 6, to_ym)
        elif k == 4:
            got(near + yp, 2)
            got(far + ym, 3)
        else:
            got(near + y2, 5)
            got(far + y2, 6)

    def part(t, col, first=0, rows=blk):
        return p[t].at[pl.ds(pl.multiple_of(col * blk + first, half), rows)]

    def block(t, k):
        return rb[t].at[pl.ds(pl.multiple_of(k * blk, blk), blk)]

    def add(ref, *others):
        total = ref[...]
        for other in others:
            total = total + other[...]
        ref[...] = total

    def sums(t, k, by_z=False):
        def out(src, dst, s, peer):
            send(src, dst, 4 + 6 * thin[t], rr_sem.at[t, s], peer)

        def got(ref, s):
            arrived(ref, rr_sem.at[t, s])

        near, far = zh * 4, (1 - zh) * 4
        if by_z and k == 0:
            out(part(t, far, 0, 4 * blk), rb[t], 6, to_zh)
        elif by_z and k == 1:
            got(rb[t], 6)
            add(part(t, near, 0, 4 * blk), rb[t])
            out(part(t, near + y2, 0, half), ra[t].at[0, pl.ds(0, half)], 0, to_yp)
            out(part(t, near + y2, half, half), ra[t].at[1, pl.ds(half, half)], 1, to_ym)
        elif by_z and k == 2:
            plus, minus = ra[t].at[0, pl.ds(0, half)], ra[t].at[1, pl.ds(half, half)]
            got(plus, 0)
            add(part(t, near + yp, 0, half), plus)
            out(part(t, near + yp), rz[t].at[0], 2, to_yp)
            got(minus, 1)
            add(part(t, near + ym, half, half), minus)
            out(part(t, near + ym), rz[t].at[1], 5, to_ym)
        elif by_z and k == 3:
            got(rz[t].at[0], 2)
            got(rz[t].at[1], 5)
            finish(t, rz[t].at[0], rz[t].at[1])
        elif by_z:
            pass
        elif k == 0:
            out(part(t, y2), ra[t].at[0], 0, to_yp)
            out(part(t, 4 + y2), ra[t].at[1], 1, to_ym)
            out(part(t, 4 + yp), block(t, 1), 3, to_yp)
            out(part(t, ym), block(t, 2), 4, to_ym)
        elif k == 1:
            got(ra[t].at[0], 0)
            add(part(t, yp), ra[t].at[0])
            out(part(t, yp), block(t, 0), 2, to_yp)
        elif k == 2:
            got(ra[t].at[1], 1)
            add(part(t, 4 + ym), ra[t].at[1])
            out(part(t, 4 + ym), block(t, 3), 5, to_ym)
        elif k == 3:
            for i in range(4):
                got(block(t, i), 2 + i)
            other = part(t, far + y)
            add(other, block(t, 1 - zh), block(t, 3 - zh))
            out(other, rz[t].at[0], 6, to_zh)
        else:
            got(rz[t].at[0], 6)
            finish(t, block(t, zh), block(t, 2 + zh), rz[t].at[0])

    def finish(t, *others):
        add(part(t, c), *others)
        m = lg[t][core, own] + part(t, c)[...]
        mc[t][core, own] = m
        mr[t][c] = m

    def rows_of(buf, t):
        for i in range(16):
            yield pl.ds(i * blk, blk), buf[t][i % 2, i // 2]

    def product_tl(t):
        arrived(lg[t].at[1 - core], rl_sem.at[t, 7])
        cols = slice(0, WIDTHS[t])
        for rows, v in rows_of(lg, t):
            hi, lo = split(v)
            l3[rows, cols] = hi
            l3[pl.ds(depth + rows.start, blk), cols] = lo
            l3[pl.ds(2 * depth + rows.start, blk), cols] = hi
        p[t][...] = jnp.dot(t3[...], l3[:, cols], preferred_element_type=F32)

    def product_mm(t):
        arrived(mc[t].at[1 - core], rm_sem.at[t, 7])
        kc = WIDTHS[t]
        for i in range(8):
            hi, lo = split(mr[t][i])
            rows = pl.ds(i * blk, blk)
            m3r[rows, :kc] = hi
            m3r[rows, kc : 2 * kc] = hi
            m3r[rows, 2 * kc : 3 * kc] = lo
        for rows, v in rows_of(mc, t):
            hi, lo = split(v)
            m3c[rows, :kc] = hi
            m3c[rows, kc : 2 * kc] = lo
            m3c[rows, 2 * kc : 3 * kc] = hi
        out_ref[...] += lax.dot_general(
            m3r[:, : 3 * kc], m3c[:, : 3 * kc], (((1,), (1,)), ((), ())), preferred_element_type=F32
        )

        if t == last:
            out_ref[...] = out_ref[...] * inv[...]

    def prepare_t():
        load_t.wait()
        hi, lo = split(tf[...])
        t3[:, :depth] = hi
        t3[:, depth : 2 * depth] = hi
        t3[:, 2 * depth :] = lo

    last = [t for name, t in SEQ if name == "X2"][-1]
    move = {
        "L": functools.partial(over_row, lg, rl_sem, 0),
        "M": functools.partial(over_row, mc, rm_sem, 2),
        "C": over_col,
        "R": sums,
    }

    def stage(name, t):
        kind, k = name[0], int(name[1])
        if name == "L0":
            pltpu.make_async_copy(l_hbm.at[:, pl.ds(0, WIDTHS[t])], lg[t].at[core, own], local_sem.at[t]).wait()
        if kind in move:
            move[kind](t, k, t in BY_Z[kind])
        elif name == "X1":
            product_tl(t)
        else:
            product_mm(t)

    for i, (name, t) in enumerate(SEQ):
        stage(name, t)
        if i == 1:
            prepare_t()

    for bufs, count, group in ((wide, counts[0], 0), (slim, counts[1], 6)):
        if count:
            for i, first in ((0, 0), (1, 2)):
                sent(bufs[i].at[:, 0, pl.ds(0, 7)], group + first)
                sent(bufs[i].at[:, 0], group + first + 1)
            sent(bufs[2].at[:, pl.ds(0, 7)], group + 4)
            sent(bufs[2].at[:, pl.ds(0, 7)], group + 5)


def shards(t_amps, cholesky, eps_occ, eps_vir):
    eps_vir = eps_vir.reshape(8, -1)
    rows, depth = t_amps.shape
    blk, chol = cholesky.shape
    assert sum(WIDTHS) == chol
    kc, n = max(WIDTHS), len(WIDTHS)
    vmem = lambda shape, dtype=F32: pltpu.VMEM(shape, dtype)
    dma = pltpu.SemaphoreType.DMA

    def buffers(count, width):
        count = max(count, 1)
        return [
            vmem((count, 2, 8, blk, width)),
            vmem((count, 2, 8, blk, width)),
            vmem((count, 8, blk, width)),
            vmem((count, rows, width)),
            vmem((count, 2, blk, width)),
            vmem((count, 4 * blk, width)),
            vmem((count, 2, blk, width)),
        ]

    return pl.pallas_call(
        kernel,
        out_shape=jax.ShapeDtypeStruct((rows, depth), F32),
        in_specs=[pl.BlockSpec(memory_space=pltpu.MemorySpace.HBM)] * 4,
        out_specs=pl.BlockSpec(memory_space=pltpu.VMEM),
        scratch_shapes=[
            buffers(sum(w == kc for w in WIDTHS), kc),
            buffers(sum(w < kc for w in WIDTHS), min(WIDTHS)),
            vmem((rows, depth)),
            vmem((rows, 3 * depth), BF16),
            vmem((3 * depth, kc), BF16),
            vmem((rows, 3 * kc), BF16),
            vmem((depth, 3 * kc), BF16),
            vmem((rows, depth)),
            pltpu.SMEM(eps_occ.shape, F32),
            vmem(eps_vir.shape),
            dma((n, 9)),
            dma((n, 9)),
            dma((n, 8)),
            dma((n, 7)),
            dma((12,)),
            dma((n + 3,)),
        ],
        compiler_params=pltpu.CompilerParams(collective_id=0, has_side_effects=True, vmem_limit_bytes=46 * 2**20),
    )(*(pltpu.with_memory_space_constraint(v, pltpu.MemorySpace.HBM) for v in (t_amps, cholesky, eps_occ, eps_vir)))


def solution(mesh):
    in_specs = (P("row", "col"), P(("row", "col"), None), P(), P())
    out_specs = P("row", "col")
    return jax.shard_map(shards, mesh=mesh, in_specs=in_specs, out_specs=out_specs, check_vma=False)
```

```python
import functools

import jax
import jax.numpy as jnp
from jax import lax
from jax.experimental import pallas as pl
from jax.experimental.pallas import tpu as pltpu
from jax.sharding import PartitionSpec as P

MESH = pl.DeviceIdType.MESH
BF16 = jnp.bfloat16
F32 = jnp.float32

SEQ = (
    ("L0", 7), ("L0", 3), ("L0", 2), ("L1", 7), ("L0", 4), ("L1", 3), ("L2", 3), ("L3", 3), ("L2", 7), ("L3", 7), ("L4", 7), ("L1", 2), ("L0", 5), ("L2", 4), ("L2", 2), ("L4", 3), ("L1", 4), ("L5", 7), ("L3", 4),
    ("L1", 5), ("L3", 2), ("X1", 7), ("L5", 3), ("L2", 5), ("R0", 7), ("L4", 4), ("L4", 2), ("L0", 1), ("X1", 3), ("R0", 3), ("L3", 5), ("L5", 2), ("L0", 6), ("L0", 0), ("L5", 4), ("R1", 7), ("R2", 7), ("X1", 2),
    ("L1", 1), ("R0", 2), ("L4", 5), ("L2", 1), ("L5", 5), ("R1", 3), ("R2", 3), ("X1", 4), ("R0", 4), ("L1", 0), ("L1", 6), ("X1", 5), ("R0", 5), ("R3", 3), ("L2", 6), ("L2", 0), ("L3", 1), ("L4", 1), ("R1", 4),
    ("R2", 4), ("R3", 7), ("L3", 0), ("L3", 6), ("R1", 2), ("L4", 0), ("L5", 1), ("R1", 5), ("R2", 5), ("R4", 3), ("M0", 3), ("L4", 6), ("C0", 3), ("L5", 0), ("X1", 1), ("R3", 4), ("R0", 1), ("R4", 7), ("R3", 5),
    ("M0", 7), ("M1", 3), ("R2", 2), ("X1", 0), ("C2", 3), ("R0", 0), ("R4", 4), ("R1", 1), ("C1", 3), ("R2", 1), ("M2", 3), ("L5", 6), ("M0", 4), ("M2", 7), ("R4", 5), ("M1", 7), ("R3", 2), ("R4", 2), ("C0", 4),
    ("C3", 3), ("M3", 3), ("M0", 5), ("X1", 6), ("R1", 0), ("R2", 0), ("M0", 2), ("R0", 6), ("C2", 4), ("C0", 2), ("M1", 4), ("M2", 4), ("R3", 0), ("C1", 4), ("M1", 2), ("R1", 6), ("R2", 6), ("R3", 1), ("M1", 5),
    ("M3", 7), ("M4", 3), ("M5", 3), ("M3", 4), ("M4", 7), ("C4", 3), ("M4", 4), ("C0", 7), ("R4", 0), ("M0", 0), ("M2", 2), ("C1", 2), ("M3", 2), ("C0", 0), ("C3", 4), ("R4", 1), ("R3", 6), ("C2", 2), ("M0", 1),
    ("C3", 2), ("C4", 4), ("M3", 5), ("C5", 3), ("M2", 5), ("C1", 7), ("X2", 3), ("C0", 1), ("M1", 0), ("C0", 5), ("C1", 0), ("R4", 6), ("M4", 2), ("M0", 6), ("M5", 7), ("M5", 2), ("C0", 6), ("M5", 4), ("C5", 4),
    ("M1", 1), ("C4", 2), ("C3", 0), ("M3", 0), ("C2", 0), ("C1", 1), ("C2", 7), ("C3", 7), ("M2", 0), ("M2", 1), ("X2", 4), ("M2", 6), ("C1", 5), ("C2", 1), ("M1", 6), ("M4", 0), ("C4", 0), ("M3", 1), ("C1", 6),
    ("C5", 2), ("X2", 2), ("C4", 7), ("C3", 1), ("M4", 1), ("M4", 5), ("M5", 0), ("M3", 6), ("C5", 7), ("X2", 7), ("C3", 5), ("M5", 1), ("C2", 5), ("C4", 5), ("C2", 6), ("M5", 5), ("C4", 1), ("C5", 0), ("M4", 6),
    ("C3", 6), ("X2", 0), ("C5", 1), ("C4", 6), ("M5", 6), ("X2", 1), ("C5", 5), ("X2", 5), ("C5", 6), ("X2", 6),
)
WIDTHS = (256, 256, 256, 256, 256, 256, 256, 256)
BY_Z = {"L": (3, 4), "M": (), "C": (0, 3), "R": (2,)}


def split(v):
    hi = v.astype(BF16)
    return hi, (v - hi.astype(F32)).astype(BF16)


def kernel(
    t_hbm, l_hbm, occ_hbm, vir_hbm, out_ref,
    wide, slim, tf, t3, l3, m3r, m3c, inv, occ, vir,
    rl_sem, rm_sem, rc_sem, rr_sem, send_sem, local_sem,
):
    n, blk = len(WIDTHS), l_hbm.shape[0]
    full = max(WIDTHS)
    counts = [0, 0]
    places = []
    for width in WIDTHS:
        kind = int(width < full)
        places.append(((wide, slim)[kind], counts[kind]))
        counts[kind] += 1
    thin = [int(width < full) for width in WIDTHS]
    lg, mc, mr, p, ra, rb, rz = ([bufs[i].at[j] for bufs, j in places] for i in range(7))
    depth = tf.shape[1]
    r, c = lax.axis_index("row"), lax.axis_index("col")
    x, zl, core = r // 4, (r // 2) % 2, r % 2
    zh, y = c // 4, c % 4
    xp, xm, x2 = (x + 1) % 4, (x + 3) % 4, (x + 2) % 4
    yp, ym, y2 = (y + 1) % 4, (y + 3) % 4, (y + 2) % 4
    to_xp, to_xm = (xp * 4 + zl * 2 + core, c), (xm * 4 + zl * 2 + core, c)
    to_z, to_core = (x * 4 + (1 - zl) * 2 + core, c), (x * 4 + zl * 2 + 1 - core, c)
    to_yp, to_ym = (r, zh * 4 + yp), (r, zh * 4 + ym)
    to_zh = (r, (1 - zh) * 4 + y)
    own = x * 2 + zl

    half = blk // 2

    barrier = pltpu.get_barrier_semaphore()
    peers = (to_xp, to_xm, to_z, to_core, to_yp, to_ym, to_zh)
    for peer in peers:
        pl.semaphore_signal(barrier, inc=1, device_id=peer, device_id_type=MESH)
    load_occ = pltpu.make_async_copy(occ_hbm, occ, local_sem.at[n + 1])
    load_vir = pltpu.make_async_copy(vir_hbm, vir, local_sem.at[n + 2])
    load_t = pltpu.make_async_copy(t_hbm, tf, local_sem.at[n])
    load_occ.start()
    load_vir.start()
    for t in range(n):
        pltpu.make_async_copy(l_hbm.at[:, pl.ds(sum(WIDTHS[:t]), WIDTHS[t])], lg[t].at[core, own], local_sem.at[t]).start()
    load_t.start()

    load_occ.wait()
    load_vir.wait()
    lanes = 2 * blk
    lane = lax.broadcasted_iota(jnp.int32, (1, lanes), 1)
    low, high = vir[pl.ds(c // 2, 1), :], vir[pl.ds(4 + c // 2, 1), :]
    even = jnp.where(lane < blk, low, pltpu.roll(high, blk, 1))
    odd = jnp.where(lane < blk, pltpu.roll(low, blk, 1), high)
    col_vir = jnp.where(c % 2 == 0, even, odd)
    for a in range(4):
        row_vir = jnp.broadcast_to(vir[pl.ds((r % 2) * 4 + a, 1), :], (lanes, lanes)).T
        row_gap = row_vir - occ[r // 2]
        for g in range(8):
            col_gap = col_vir - occ[g]
            inv[pl.ds(a * lanes, lanes), pl.ds(g * lanes, lanes)] = -1.0 / (row_gap + col_gap)
    out_ref[...] = jnp.zeros_like(out_ref)

    pl.semaphore_wait(barrier, len(peers))

    def send(src, dst, group, arrive, peer):
        pltpu.make_async_remote_copy(
            src_ref=src, dst_ref=dst, send_sem=send_sem.at[group], recv_sem=arrive, device_id=peer, device_id_type=MESH
        ).start()

    def arrived(ref, sem):
        pltpu.make_async_remote_copy(
            src_ref=ref, dst_ref=ref, send_sem=send_sem.at[0], recv_sem=sem, device_id=to_core, device_id_type=MESH
        ).wait_recv()

    def sent(ref, group):
        pltpu.make_async_remote_copy(
            src_ref=ref, dst_ref=ref, send_sem=send_sem.at[group], recv_sem=rr_sem.at[0, 0], device_id=to_core, device_id_type=MESH
        ).wait_send()

    def over_row(buf, sem, group, t, k, by_z=False):
        def at(slot):
            return buf[t].at[core, slot]

        def out(slot, s, peer):
            send(at(slot), at(slot), group + 6 * thin[t], sem.at[t, s], peer)

        def share(slot):
            send(at(slot), at(slot), group + 1 + 6 * thin[t], sem.at[t, 7], to_core)

        def got(slot, s):
            arrived(at(slot), sem.at[t, s])

        def pass_on(slot, first, s, peer):
            ref = at(slot).at[pl.ds(first, half)]
            send(ref, ref, group + 6 * thin[t], sem.at[t, s], peer)

        near, far = zl, 1 - zl
        if by_z and k == 0:
            out(own, 1, to_xp)
            out(own, 2, to_xm)
            out(own, 0, to_z)
            share(own)
        elif by_z and k == 1:
            got(x * 2 + far, 0)
            share(x * 2 + far)
        elif by_z and k == 2:
            got(xm * 2 + near, 1)
            pass_on(xm * 2 + near, 0, 5, to_xp)
            out(xm * 2 + near, 3, to_z)
            share(xm * 2 + near)
        elif by_z and k == 3:
            got(xp * 2 + near, 2)
            pass_on(xp * 2 + near, half, 6, to_xm)
            out(xp * 2 + near, 4, to_z)
            share(xp * 2 + near)
        elif by_z and k == 4:
            arrived(at(x2 * 2 + near).at[pl.ds(0, half)], sem.at[t, 5])
            arrived(at(x2 * 2 + near).at[pl.ds(half, half)], sem.at[t, 6])
            out(x2 * 2 + near, 8, to_z)
            share(x2 * 2 + near)
        elif by_z:
            for slot, s in ((xm, 3), (xp, 4), (x2, 8)):
                got(slot * 2 + far, s)
                share(slot * 2 + far)
        elif k == 0:
            out(own, 0, to_z)
            out(own, 1, to_xp)
            out(own, 2, to_xm)
            share(own)
        elif k == 1:
            mate = x * 2 + far
            got(mate, 0)
            out(mate, 3, to_xp)
            out(mate, 4, to_xm)
            share(mate)
        elif k == 2:
            got(xm * 2 + near, 1)
            out(xm * 2 + near, 5, to_xp)
            share(xm * 2 + near)
        elif k == 3:
            got(xp * 2 + far, 4)
            out(xp * 2 + far, 6, to_xm)
            share(xp * 2 + far)
        elif k == 4:
            got(xp * 2 + near, 2)
            share(xp * 2 + near)
            got(xm * 2 + far, 3)
            share(xm * 2 + far)
        else:
            got(x2 * 2 + near, 5)
            share(x2 * 2 + near)
            got(x2 * 2 + far, 6)
            share(x2 * 2 + far)

    def over_col(t, k, by_z=False):
        def out(slot, s, peer):
            send(mr[t].at[slot], mr[t].at[slot], 5 + 6 * thin[t], rc_sem.at[t, s], peer)

        def got(slot, s):
            arrived(mr[t].at[slot], rc_sem.at[t, s])

        def pass_on(slot, first, s, peer):
            ref = mr[t].at[slot, pl.ds(first, half)]
            send(ref, ref, 5 + 6 * thin[t], rc_sem.at[t, s], peer)

        near, far = zh * 4, (1 - zh) * 4
        if by_z and k == 0:
            out(c, 1, to_yp)
            out(c, 2, to_ym)
            out(c, 0, to_zh)
        elif by_z and k == 1:
            got(far + y, 0)
        elif by_z and k == 2:
            got(near + ym, 1)
            pass_on(near + ym, 0, 5, to_yp)
            out(near + ym, 3, to_zh)
        elif by_z and k == 3:
            got(near + yp, 2)
            pass_on(near + yp, half, 6, to_ym)
            out(near + yp, 4, to_zh)
        elif by_z and k == 4:
            arrived(mr[t].at[near + y2, pl.ds(0, half)], rc_sem.at[t, 5])
            arrived(mr[t].at[near + y2, pl.ds(half, half)], rc_sem.at[t, 6])
            out(near + y2, 7, to_zh)
        elif by_z:
            for slot, s in ((ym, 3), (yp, 4), (y2, 7)):
                got(far + slot, s)
        elif k == 0:
            out(c, 0, to_zh)
            out(c, 1, to_yp)
            out(c, 2, to_ym)
        elif k == 1:
            got(far + y, 0)
            out(far + y, 3, to_yp)
            out(far + y, 4, to_ym)
        elif k == 2:
            got(near + ym, 1)
            out(near + ym, 5, to_yp)
        elif k == 3:
            got(far + yp, 4)
            out(far + yp, 6, to_ym)
        elif k == 4:
            got(near + yp, 2)
            got(far + ym, 3)
        else:
            got(near + y2, 5)
            got(far + y2, 6)

    def part(t, col, first=0, rows=blk):
        return p[t].at[pl.ds(pl.multiple_of(col * blk + first, half), rows)]

    def block(t, k):
        return rb[t].at[pl.ds(pl.multiple_of(k * blk, blk), blk)]

    def add(ref, *others):
        total = ref[...]
        for other in others:
            total = total + other[...]
        ref[...] = total

    def sums(t, k, by_z=False):
        def out(src, dst, s, peer):
            send(src, dst, 4 + 6 * thin[t], rr_sem.at[t, s], peer)

        def got(ref, s):
            arrived(ref, rr_sem.at[t, s])

        near, far = zh * 4, (1 - zh) * 4
        if by_z and k == 0:
            out(part(t, far, 0, 4 * blk), rb[t], 6, to_zh)
        elif by_z and k == 1:
            got(rb[t], 6)
            add(part(t, near, 0, 4 * blk), rb[t])
            out(part(t, near + y2, 0, half), ra[t].at[0, pl.ds(0, half)], 0, to_yp)
            out(part(t, near + y2, half, half), ra[t].at[1, pl.ds(half, half)], 1, to_ym)
        elif by_z and k == 2:
            plus, minus = ra[t].at[0, pl.ds(0, half)], ra[t].at[1, pl.ds(half, half)]
            got(plus, 0)
            add(part(t, near + yp, 0, half), plus)
            out(part(t, near + yp), rz[t].at[0], 2, to_yp)
            got(minus, 1)
            add(part(t, near + ym, half, half), minus)
            out(part(t, near + ym), rz[t].at[1], 5, to_ym)
        elif by_z and k == 3:
            got(rz[t].at[0], 2)
            got(rz[t].at[1], 5)
            finish(t, rz[t].at[0], rz[t].at[1])
        elif by_z:
            pass
        elif k == 0:
            out(part(t, y2), ra[t].at[0], 0, to_yp)
            out(part(t, 4 + y2), ra[t].at[1], 1, to_ym)
            out(part(t, 4 + yp), block(t, 1), 3, to_yp)
            out(part(t, ym), block(t, 2), 4, to_ym)
        elif k == 1:
            got(ra[t].at[0], 0)
            add(part(t, yp), ra[t].at[0])
            out(part(t, yp), block(t, 0), 2, to_yp)
        elif k == 2:
            got(ra[t].at[1], 1)
            add(part(t, 4 + ym), ra[t].at[1])
            out(part(t, 4 + ym), block(t, 3), 5, to_ym)
        elif k == 3:
            for i in range(4):
                got(block(t, i), 2 + i)
            other = part(t, far + y)
            add(other, block(t, 1 - zh), block(t, 3 - zh))
            out(other, rz[t].at[0], 6, to_zh)
        else:
            got(rz[t].at[0], 6)
            finish(t, block(t, zh), block(t, 2 + zh), rz[t].at[0])

    def finish(t, *others):
        add(part(t, c), *others)
        m = lg[t][core, own] + part(t, c)[...]
        mc[t][core, own] = m
        mr[t][c] = m

    def rows_of(buf, t):
        for i in range(16):
            yield pl.ds(i * blk, blk), buf[t][i % 2, i // 2]

    def product_tl(t):
        arrived(lg[t].at[1 - core], rl_sem.at[t, 7])
        cols = slice(0, WIDTHS[t])
        for rows, v in rows_of(lg, t):
            hi, lo = split(v)
            l3[rows, cols] = hi
            l3[pl.ds(depth + rows.start, blk), cols] = lo
            l3[pl.ds(2 * depth + rows.start, blk), cols] = hi
        p[t][...] = jnp.dot(t3[...], l3[:, cols], preferred_element_type=F32)

    def product_mm(t):
        arrived(mc[t].at[1 - core], rm_sem.at[t, 7])
        kc = WIDTHS[t]
        for i in range(8):
            hi, lo = split(mr[t][i])
            rows = pl.ds(i * blk, blk)
            m3r[rows, :kc] = hi
            m3r[rows, kc : 2 * kc] = hi
            m3r[rows, 2 * kc : 3 * kc] = lo
        for rows, v in rows_of(mc, t):
            hi, lo = split(v)
            m3c[rows, :kc] = hi
            m3c[rows, kc : 2 * kc] = lo
            m3c[rows, 2 * kc : 3 * kc] = hi
        out_ref[...] += lax.dot_general(
            m3r[:, : 3 * kc], m3c[:, : 3 * kc], (((1,), (1,)), ((), ())), preferred_element_type=F32
        )

        if t == last:
            out_ref[...] = out_ref[...] * inv[...]

    def prepare_t():
        load_t.wait()
        hi, lo = split(tf[...])
        t3[:, :depth] = hi
        t3[:, depth : 2 * depth] = hi
        t3[:, 2 * depth :] = lo

    last = [t for name, t in SEQ if name == "X2"][-1]
    move = {
        "L": functools.partial(over_row, lg, rl_sem, 0),
        "M": functools.partial(over_row, mc, rm_sem, 2),
        "C": over_col,
        "R": sums,
    }

    def stage(name, t):
        kind, k = name[0], int(name[1])
        if name == "L0":
            pltpu.make_async_copy(l_hbm.at[:, pl.ds(0, WIDTHS[t])], lg[t].at[core, own], local_sem.at[t]).wait()
        if kind in move:
            move[kind](t, k, t in BY_Z[kind])
        elif name == "X1":
            product_tl(t)
        else:
            product_mm(t)

    for i, (name, t) in enumerate(SEQ):
        stage(name, t)
        if i == 1:
            prepare_t()

    for bufs, count, group in ((wide, counts[0], 0), (slim, counts[1], 6)):
        if count:
            for i, first in ((0, 0), (1, 2)):
                sent(bufs[i].at[:, 0, pl.ds(0, 7)], group + first)
                sent(bufs[i].at[:, 0], group + first + 1)
            sent(bufs[2].at[:, pl.ds(0, 7)], group + 4)
            sent(bufs[2].at[:, pl.ds(0, 7)], group + 5)


def shards(t_amps, cholesky, eps_occ, eps_vir):
    eps_vir = eps_vir.reshape(8, -1)
    rows, depth = t_amps.shape
    blk, chol = cholesky.shape
    assert sum(WIDTHS) == chol
    kc, n = max(WIDTHS), len(WIDTHS)
    vmem = lambda shape, dtype=F32: pltpu.VMEM(shape, dtype)
    dma = pltpu.SemaphoreType.DMA

    def buffers(count, width):
        count = max(count, 1)
        return [
            vmem((count, 2, 8, blk, width)),
            vmem((count, 2, 8, blk, width)),
            vmem((count, 8, blk, width)),
            vmem((count, rows, width)),
            vmem((count, 2, blk, width)),
            vmem((count, 4 * blk, width)),
            vmem((count, 2, blk, width)),
        ]

    return pl.pallas_call(
        kernel,
        out_shape=jax.ShapeDtypeStruct((rows, depth), F32),
        in_specs=[pl.BlockSpec(memory_space=pltpu.MemorySpace.HBM)] * 4,
        out_specs=pl.BlockSpec(memory_space=pltpu.VMEM),
        scratch_shapes=[
            buffers(sum(w == kc for w in WIDTHS), kc),
            buffers(sum(w < kc for w in WIDTHS), min(WIDTHS)),
            vmem((rows, depth)),
            vmem((rows, 3 * depth), BF16),
            vmem((3 * depth, kc), BF16),
            vmem((rows, 3 * kc), BF16),
            vmem((depth, 3 * kc), BF16),
            vmem((rows, depth)),
            pltpu.SMEM(eps_occ.shape, F32),
            vmem(eps_vir.shape),
            dma((n, 9)),
            dma((n, 9)),
            dma((n, 8)),
            dma((n, 7)),
            dma((12,)),
            dma((n + 3,)),
        ],
        compiler_params=pltpu.CompilerParams(collective_id=0, has_side_effects=True, vmem_limit_bytes=46 * 2**20),
    )(*(pltpu.with_memory_space_constraint(v, pltpu.MemorySpace.HBM) for v in (t_amps, cholesky, eps_occ, eps_vir)))


def solution(mesh):
    in_specs = (P("row", "col"), P(("row", "col"), None), P(), P())
    out_specs = P("row", "col")
    return jax.shard_map(shards, mesh=mesh, in_specs=in_specs, out_specs=out_specs, check_vma=False)
```

```python
import functools

import jax
import jax.numpy as jnp
from jax import lax
from jax.experimental import pallas as pl
from jax.experimental.pallas import tpu as pltpu
from jax.sharding import PartitionSpec as P

MESH = pl.DeviceIdType.MESH
BF16 = jnp.bfloat16
F32 = jnp.float32

SEQ = (
    ("L0", 3), ("L0", 5), ("L0", 6), ("L1", 3), ("L0", 2), ("L2", 5), ("L2", 3), ("L1", 5), ("L3", 5), ("L3", 3), ("L0", 7), ("L1", 6), ("L3", 6), ("L4", 5), ("L4", 3), ("L2", 6), ("L1", 2), ("L5", 3), ("L1", 7),
    ("X1", 3), ("L4", 6), ("L0", 4), ("R0", 3), ("L5", 5), ("L2", 2), ("L2", 7), ("L3", 2), ("L0", 0), ("X1", 5), ("R0", 5), ("L3", 7), ("L5", 6), ("L4", 2), ("R1", 3), ("R2", 3), ("L4", 7), ("L5", 2), ("L1", 4),
    ("X1", 6), ("R0", 6), ("L1", 0), ("L5", 7), ("L2", 4), ("L0", 1), ("L2", 0), ("X1", 2), ("R0", 2), ("R3", 3), ("L3", 4), ("X1", 7), ("R0", 7), ("L4", 4), ("R1", 6), ("R2", 6), ("R1", 5), ("R2", 5), ("L3", 0),
    ("L5", 4), ("L4", 0), ("R1", 2), ("R4", 3), ("R2", 2), ("C0", 3), ("L5", 0), ("L1", 1), ("X1", 4), ("R3", 6), ("R0", 4), ("M0", 3), ("X1", 0), ("R3", 5), ("R3", 2), ("L2", 1), ("R0", 0), ("R1", 7), ("L3", 1),
    ("R1", 4), ("L4", 1), ("R2", 4), ("R4", 6), ("C0", 6), ("M0", 6), ("R1", 0), ("M1", 3), ("R4", 5), ("R2", 0), ("L5", 1), ("M0", 5), ("R4", 2), ("R2", 7), ("M0", 2), ("R3", 4), ("C0", 5), ("M2", 6), ("X1", 1),
    ("R0", 1), ("M3", 3), ("M1", 6), ("R3", 0), ("R3", 7), ("M1", 5), ("R4", 7), ("C1", 6), ("C0", 7), ("M0", 7), ("R1", 1), ("M1", 2), ("R2", 1), ("C0", 2), ("R4", 0), ("M0", 0), ("M3", 6), ("M4", 6), ("C0", 0),
    ("C3", 6), ("M2", 5), ("R4", 4), ("M2", 3), ("M1", 7), ("M0", 4), ("C1", 3), ("C2", 5), ("M2", 0), ("R3", 1), ("M3", 5), ("C2", 6), ("C1", 5), ("C2", 3), ("M1", 0), ("C0", 4), ("C3", 3), ("C4", 6), ("M3", 7),
    ("C1", 0), ("C3", 5), ("M4", 5), ("M2", 7), ("M1", 4), ("M2", 2), ("R4", 1), ("M0", 1), ("C4", 5), ("C0", 1), ("M3", 0), ("M4", 7), ("M5", 5), ("C1", 7), ("C4", 3), ("C2", 7), ("C3", 7), ("M4", 3), ("C1", 4),
    ("C3", 0), ("M2", 4), ("M5", 6), ("C1", 2), ("C2", 0), ("M1", 1), ("M3", 4), ("M3", 2), ("C4", 0), ("M5", 3), ("C5", 5), ("X2", 5), ("C2", 2), ("C2", 4), ("M4", 2), ("C4", 7), ("C5", 6), ("C1", 1), ("M5", 7),
    ("M4", 0), ("M4", 4), ("X2", 6), ("C2", 1), ("C5", 3), ("M5", 0), ("M2", 1), ("C3", 4), ("M3", 1), ("X2", 3), ("C4", 4), ("C3", 2), ("C5", 0), ("M5", 4), ("X2", 0), ("M4", 1), ("M5", 2), ("C3", 1), ("C5", 7),
    ("X2", 7), ("C4", 2), ("C5", 4), ("M5", 1), ("X2", 4), ("C5", 2), ("X2", 2), ("C4", 1), ("C5", 1), ("X2", 1),
)
WIDTHS = (256, 256, 256, 256, 256, 256, 256, 256)
BY_Z = {"L": (5, 6), "M": (), "C": (3, 7), "R": (7,)}


def split(v):
    hi = v.astype(BF16)
    return hi, (v - hi.astype(F32)).astype(BF16)


def kernel(
    t_hbm, l_hbm, occ_hbm, vir_hbm, out_ref,
    wide, slim, tf, t3, l3, m3r, m3c, inv, occ, vir,
    rl_sem, rm_sem, rc_sem, rr_sem, send_sem, local_sem,
):
    n, blk = len(WIDTHS), l_hbm.shape[0]
    full = max(WIDTHS)
    counts = [0, 0]
    places = []
    for width in WIDTHS:
        kind = int(width < full)
        places.append(((wide, slim)[kind], counts[kind]))
        counts[kind] += 1
    thin = [int(width < full) for width in WIDTHS]
    lg, mc, mr, p, ra, rb, rz = ([bufs[i].at[j] for bufs, j in places] for i in range(7))
    depth = tf.shape[1]
    r, c = lax.axis_index("row"), lax.axis_index("col")
    x, zl, core = r // 4, (r // 2) % 2, r % 2
    zh, y = c // 4, c % 4
    xp, xm, x2 = (x + 1) % 4, (x + 3) % 4, (x + 2) % 4
    yp, ym, y2 = (y + 1) % 4, (y + 3) % 4, (y + 2) % 4
    to_xp, to_xm = (xp * 4 + zl * 2 + core, c), (xm * 4 + zl * 2 + core, c)
    to_z, to_core = (x * 4 + (1 - zl) * 2 + core, c), (x * 4 + zl * 2 + 1 - core, c)
    to_yp, to_ym = (r, zh * 4 + yp), (r, zh * 4 + ym)
    to_zh = (r, (1 - zh) * 4 + y)
    own = x * 2 + zl

    half = blk // 2

    barrier = pltpu.get_barrier_semaphore()
    peers = (to_xp, to_xm, to_z, to_core, to_yp, to_ym, to_zh)
    for peer in peers:
        pl.semaphore_signal(barrier, inc=1, device_id=peer, device_id_type=MESH)
    load_occ = pltpu.make_async_copy(occ_hbm, occ, local_sem.at[n + 1])
    load_vir = pltpu.make_async_copy(vir_hbm, vir, local_sem.at[n + 2])
    load_t = pltpu.make_async_copy(t_hbm, tf, local_sem.at[n])
    load_occ.start()
    load_vir.start()
    for t in range(n):
        pltpu.make_async_copy(l_hbm.at[:, pl.ds(sum(WIDTHS[:t]), WIDTHS[t])], lg[t].at[core, own], local_sem.at[t]).start()
    load_t.start()

    pl.semaphore_wait(barrier, len(peers))

    def send(src, dst, group, arrive, peer):
        pltpu.make_async_remote_copy(
            src_ref=src, dst_ref=dst, send_sem=send_sem.at[group], recv_sem=arrive, device_id=peer, device_id_type=MESH
        ).start()

    def arrived(ref, sem):
        pltpu.make_async_remote_copy(
            src_ref=ref, dst_ref=ref, send_sem=send_sem.at[0], recv_sem=sem, device_id=to_core, device_id_type=MESH
        ).wait_recv()

    def sent(ref, group):
        pltpu.make_async_remote_copy(
            src_ref=ref, dst_ref=ref, send_sem=send_sem.at[group], recv_sem=rr_sem.at[0, 0], device_id=to_core, device_id_type=MESH
        ).wait_send()

    def over_row(buf, sem, group, t, k, by_z=False):
        def at(slot):
            return buf[t].at[core, slot]

        def out(slot, s, peer):
            send(at(slot), at(slot), group + 6 * thin[t], sem.at[t, s], peer)

        def share(slot):
            send(at(slot), at(slot), group + 1 + 6 * thin[t], sem.at[t, 7], to_core)

        def got(slot, s):
            arrived(at(slot), sem.at[t, s])

        def pass_on(slot, first, s, peer):
            ref = at(slot).at[pl.ds(first, half)]
            send(ref, ref, group + 6 * thin[t], sem.at[t, s], peer)

        near, far = zl, 1 - zl
        if by_z and k == 0:
            out(own, 1, to_xp)
            out(own, 2, to_xm)
            out(own, 0, to_z)
            share(own)
        elif by_z and k == 1:
            got(x * 2 + far, 0)
            share(x * 2 + far)
        elif by_z and k == 2:
            got(xm * 2 + near, 1)
            pass_on(xm * 2 + near, 0, 5, to_xp)
            out(xm * 2 + near, 3, to_z)
            share(xm * 2 + near)
        elif by_z and k == 3:
            got(xp * 2 + near, 2)
            pass_on(xp * 2 + near, half, 6, to_xm)
            out(xp * 2 + near, 4, to_z)
            share(xp * 2 + near)
        elif by_z and k == 4:
            arrived(at(x2 * 2 + near).at[pl.ds(0, half)], sem.at[t, 5])
            arrived(at(x2 * 2 + near).at[pl.ds(half, half)], sem.at[t, 6])
            out(x2 * 2 + near, 8, to_z)
            share(x2 * 2 + near)
        elif by_z:
            for slot, s in ((xm, 3), (xp, 4), (x2, 8)):
                got(slot * 2 + far, s)
                share(slot * 2 + far)
        elif k == 0:
            out(own, 0, to_z)
            out(own, 1, to_xp)
            out(own, 2, to_xm)
            share(own)
        elif k == 1:
            mate = x * 2 + far
            got(mate, 0)
            out(mate, 3, to_xp)
            out(mate, 4, to_xm)
            share(mate)
        elif k == 2:
            got(xm * 2 + near, 1)
            out(xm * 2 + near, 5, to_xp)
            share(xm * 2 + near)
        elif k == 3:
            got(xp * 2 + far, 4)
            out(xp * 2 + far, 6, to_xm)
            share(xp * 2 + far)
        elif k == 4:
            got(xp * 2 + near, 2)
            share(xp * 2 + near)
            got(xm * 2 + far, 3)
            share(xm * 2 + far)
        else:
            got(x2 * 2 + near, 5)
            share(x2 * 2 + near)
            got(x2 * 2 + far, 6)
            share(x2 * 2 + far)

    def over_col(t, k, by_z=False):
        def out(slot, s, peer):
            send(mr[t].at[slot], mr[t].at[slot], 5 + 6 * thin[t], rc_sem.at[t, s], peer)

        def got(slot, s):
            arrived(mr[t].at[slot], rc_sem.at[t, s])

        def pass_on(slot, first, s, peer):
            ref = mr[t].at[slot, pl.ds(first, half)]
            send(ref, ref, 5 + 6 * thin[t], rc_sem.at[t, s], peer)

        near, far = zh * 4, (1 - zh) * 4
        if by_z and k == 0:
            out(c, 1, to_yp)
            out(c, 2, to_ym)
            out(c, 0, to_zh)
        elif by_z and k == 1:
            got(far + y, 0)
        elif by_z and k == 2:
            got(near + ym, 1)
            pass_on(near + ym, 0, 5, to_yp)
            out(near + ym, 3, to_zh)
        elif by_z and k == 3:
            got(near + yp, 2)
            pass_on(near + yp, half, 6, to_ym)
            out(near + yp, 4, to_zh)
        elif by_z and k == 4:
            arrived(mr[t].at[near + y2, pl.ds(0, half)], rc_sem.at[t, 5])
            arrived(mr[t].at[near + y2, pl.ds(half, half)], rc_sem.at[t, 6])
            out(near + y2, 7, to_zh)
        elif by_z:
            for slot, s in ((ym, 3), (yp, 4), (y2, 7)):
                got(far + slot, s)
        elif k == 0:
            out(c, 0, to_zh)
            out(c, 1, to_yp)
            out(c, 2, to_ym)
        elif k == 1:
            got(far + y, 0)
            out(far + y, 3, to_yp)
            out(far + y, 4, to_ym)
        elif k == 2:
            got(near + ym, 1)
            out(near + ym, 5, to_yp)
        elif k == 3:
            got(far + yp, 4)
            out(far + yp, 6, to_ym)
        elif k == 4:
            got(near + yp, 2)
            got(far + ym, 3)
        else:
            got(near + y2, 5)
            got(far + y2, 6)

    def part(t, col, first=0, rows=blk):
        return p[t].at[pl.ds(pl.multiple_of(col * blk + first, half), rows)]

    def block(t, k):
        return rb[t].at[pl.ds(pl.multiple_of(k * blk, blk), blk)]

    def add(ref, *others):
        total = ref[...]
        for other in others:
            total = total + other[...]
        ref[...] = total

    def sums(t, k, by_z=False):
        def out(src, dst, s, peer):
            send(src, dst, 4 + 6 * thin[t], rr_sem.at[t, s], peer)

        def got(ref, s):
            arrived(ref, rr_sem.at[t, s])

        near, far = zh * 4, (1 - zh) * 4
        if by_z and k == 0:
            out(part(t, far, 0, 4 * blk), rb[t], 6, to_zh)
        elif by_z and k == 1:
            got(rb[t], 6)
            add(part(t, near, 0, 4 * blk), rb[t])
            out(part(t, near + y2, 0, half), ra[t].at[0, pl.ds(0, half)], 0, to_yp)
            out(part(t, near + y2, half, half), ra[t].at[1, pl.ds(half, half)], 1, to_ym)
        elif by_z and k == 2:
            plus, minus = ra[t].at[0, pl.ds(0, half)], ra[t].at[1, pl.ds(half, half)]
            got(plus, 0)
            add(part(t, near + yp, 0, half), plus)
            out(part(t, near + yp), rz[t].at[0], 2, to_yp)
            got(minus, 1)
            add(part(t, near + ym, half, half), minus)
            out(part(t, near + ym), rz[t].at[1], 5, to_ym)
        elif by_z and k == 3:
            got(rz[t].at[0], 2)
            got(rz[t].at[1], 5)
            finish(t, rz[t].at[0], rz[t].at[1])
        elif by_z:
            pass
        elif k == 0:
            out(part(t, y2), ra[t].at[0], 0, to_yp)
            out(part(t, 4 + y2), ra[t].at[1], 1, to_ym)
            out(part(t, 4 + yp), block(t, 1), 3, to_yp)
            out(part(t, ym), block(t, 2), 4, to_ym)
        elif k == 1:
            got(ra[t].at[0], 0)
            add(part(t, yp), ra[t].at[0])
            out(part(t, yp), block(t, 0), 2, to_yp)
        elif k == 2:
            got(ra[t].at[1], 1)
            add(part(t, 4 + ym), ra[t].at[1])
            out(part(t, 4 + ym), block(t, 3), 5, to_ym)
        elif k == 3:
            for i in range(4):
                got(block(t, i), 2 + i)
            other = part(t, far + y)
            add(other, block(t, 1 - zh), block(t, 3 - zh))
            out(other, rz[t].at[0], 6, to_zh)
        else:
            got(rz[t].at[0], 6)
            finish(t, block(t, zh), block(t, 2 + zh), rz[t].at[0])

    def finish(t, *others):
        add(part(t, c), *others)
        m = lg[t][core, own] + part(t, c)[...]
        mc[t][core, own] = m
        mr[t][c] = m

    def rows_of(buf, t):
        for i in range(16):
            yield pl.ds(i * blk, blk), buf[t][i % 2, i // 2]

    def product_tl(t):
        arrived(lg[t].at[1 - core], rl_sem.at[t, 7])
        cols = slice(0, WIDTHS[t])
        for rows, v in rows_of(lg, t):
            hi, lo = split(v)
            l3[rows, cols] = hi
            l3[pl.ds(depth + rows.start, blk), cols] = lo
            l3[pl.ds(2 * depth + rows.start, blk), cols] = hi
        p[t][...] = jnp.dot(t3[...], l3[:, cols], preferred_element_type=F32)

    def product_mm(t):
        arrived(mc[t].at[1 - core], rm_sem.at[t, 7])
        kc = WIDTHS[t]
        for i in range(8):
            hi, lo = split(mr[t][i])
            rows = pl.ds(i * blk, blk)
            m3r[rows, :kc] = hi
            m3r[rows, kc : 2 * kc] = hi
            m3r[rows, 2 * kc : 3 * kc] = lo
        for rows, v in rows_of(mc, t):
            hi, lo = split(v)
            m3c[rows, :kc] = hi
            m3c[rows, kc : 2 * kc] = lo
            m3c[rows, 2 * kc : 3 * kc] = hi
        total = out_ref[...] + lax.dot_general(
            m3r[:, : 3 * kc], m3c[:, : 3 * kc], (((1,), (1,)), ((), ())), preferred_element_type=F32
        )
        out_ref[...] = total * inv[...] if t == last else total

    def prepare_gaps():
        load_occ.wait()
        load_vir.wait()
        lanes = 2 * blk
        lane = lax.broadcasted_iota(jnp.int32, (1, lanes), 1)
        low, high = vir[pl.ds(c // 2, 1), :], vir[pl.ds(4 + c // 2, 1), :]
        even = jnp.where(lane < blk, low, pltpu.roll(high, blk, 1))
        odd = jnp.where(lane < blk, pltpu.roll(low, blk, 1), high)
        col_vir = jnp.where(c % 2 == 0, even, odd)
        for a in range(4):
            row_vir = jnp.broadcast_to(vir[pl.ds((r % 2) * 4 + a, 1), :], (lanes, lanes)).T
            row_gap = row_vir - occ[r // 2]
            for g in range(8):
                col_gap = col_vir - occ[g]
                inv[pl.ds(a * lanes, lanes), pl.ds(g * lanes, lanes)] = -1.0 / (row_gap + col_gap)
        out_ref[...] = jnp.zeros_like(out_ref)

    def prepare_t():
        load_t.wait()
        hi, lo = split(tf[...])
        t3[:, :depth] = hi
        t3[:, depth : 2 * depth] = hi
        t3[:, 2 * depth :] = lo

    last = [t for name, t in SEQ if name == "X2"][-1]
    move = {
        "L": functools.partial(over_row, lg, rl_sem, 0),
        "M": functools.partial(over_row, mc, rm_sem, 2),
        "C": over_col,
        "R": sums,
    }

    def stage(name, t):
        kind, k = name[0], int(name[1])
        if name == "L0":
            pltpu.make_async_copy(l_hbm.at[:, pl.ds(0, WIDTHS[t])], lg[t].at[core, own], local_sem.at[t]).wait()
        if kind in move:
            move[kind](t, k, t in BY_Z[kind])
        elif name == "X1":
            product_tl(t)
        else:
            product_mm(t)

    for i, (name, t) in enumerate(SEQ):
        stage(name, t)
        if i == 1:
            prepare_t()
            prepare_gaps()

    for bufs, count, group in ((wide, counts[0], 0), (slim, counts[1], 6)):
        if count:
            for i, first in ((0, 0), (1, 2)):
                sent(bufs[i].at[:, 0, pl.ds(0, 7)], group + first)
                sent(bufs[i].at[:, 0], group + first + 1)
            sent(bufs[2].at[:, pl.ds(0, 7)], group + 4)
            sent(bufs[2].at[:, pl.ds(0, 7)], group + 5)


def shards(t_amps, cholesky, eps_occ, eps_vir):
    eps_vir = eps_vir.reshape(8, -1)
    rows, depth = t_amps.shape
    blk, chol = cholesky.shape
    assert sum(WIDTHS) == chol
    kc, n = max(WIDTHS), len(WIDTHS)
    vmem = lambda shape, dtype=F32: pltpu.VMEM(shape, dtype)
    dma = pltpu.SemaphoreType.DMA

    def buffers(count, width):
        count = max(count, 1)
        return [
            vmem((count, 2, 8, blk, width)),
            vmem((count, 2, 8, blk, width)),
            vmem((count, 8, blk, width)),
            vmem((count, rows, width)),
            vmem((count, 2, blk, width)),
            vmem((count, 4 * blk, width)),
            vmem((count, 2, blk, width)),
        ]

    return pl.pallas_call(
        kernel,
        out_shape=jax.ShapeDtypeStruct((rows, depth), F32),
        in_specs=[pl.BlockSpec(memory_space=pltpu.MemorySpace.HBM)] * 4,
        out_specs=pl.BlockSpec(memory_space=pltpu.VMEM),
        scratch_shapes=[
            buffers(sum(w == kc for w in WIDTHS), kc),
            buffers(sum(w < kc for w in WIDTHS), min(WIDTHS)),
            vmem((rows, depth)),
            vmem((rows, 3 * depth), BF16),
            vmem((3 * depth, kc), BF16),
            vmem((rows, 3 * kc), BF16),
            vmem((depth, 3 * kc), BF16),
            vmem((rows, depth)),
            pltpu.SMEM(eps_occ.shape, F32),
            vmem(eps_vir.shape),
            dma((n, 9)),
            dma((n, 9)),
            dma((n, 8)),
            dma((n, 7)),
            dma((12,)),
            dma((n + 3,)),
        ],
        compiler_params=pltpu.CompilerParams(collective_id=0, has_side_effects=True, vmem_limit_bytes=46 * 2**20),
    )(*(pltpu.with_memory_space_constraint(v, pltpu.MemorySpace.HBM) for v in (t_amps, cholesky, eps_occ, eps_vir)))


def solution(mesh):
    in_specs = (P("row", "col"), P(("row", "col"), None), P(), P())
    out_specs = P("row", "col")
    return jax.shard_map(shards, mesh=mesh, in_specs=in_specs, out_specs=out_specs, check_vma=False)
```
